128 devices in a mesh: fsdp: 4 (over z), tp: 32 (over y, x, core).
Axes of the slice: x: 4, y: 4, z: 4, core: 2. Of those that a mesh axis runs over, the one named last changes fastest.
Arguments:
- inputs: bfloat16 [2048, 4096], P('fsdp'), may hold values from -6 to 6
- out_grad: bfloat16 [2048, 4096], P('fsdp'), may hold values from -6 to 6
- gate_tiles: bfloat16 [32, 16, 128, 128], P('tp', 'fsdp'), may hold values from -0.25 to 0.25
- up_tiles: bfloat16 [32, 16, 128, 128], P('tp', 'fsdp'), may hold values from -0.25 to 0.25
- down_tiles: bfloat16 [32, 16, 128, 128], P('tp', 'fsdp'), may hold values from -0.125 to 0.125
- in_rows: int32 [32, 16], P('tp'), may hold values from 0 to 31, as said below
- in_cols: int32 [32, 16], P('tp'), may hold values from 0 to 3
- down_rows: int32 [32, 16], P('tp'), may hold values from 0 to 3, as said below
- down_cols: int32 [32, 16], P('tp'), may hold values from 0 to 31
Outputs:
- ffn_out: bfloat16 [2048, 4096], P('fsdp', 'tp')
- input_grad: bfloat16 [2048, 4096], P('fsdp', 'tp')
- gate_grad: float32 [32, 16, 128, 128], P('tp', 'fsdp')
- up_grad: float32 [32, 16, 128, 128], P('tp', 'fsdp')
- down_grad: float32 [32, 16, 128, 128], P('tp', 'fsdp')
The draws below stay inside these ranges and needn't reach their ends.
Inputs may be any that keep to these rules, and one draw needn't show every extreme that they name: For each index of the first dimension, the pairs (in_rows, in_cols) are distinct. For each index of the first dimension, the pairs (down_rows, down_cols) are distinct.
All inputs are finite; a program needn't handle non-finite values.
Results may differ from the reference program's by a relative error of at most 0.014.
Values may be sent and summed in bfloat16 or wider, within the bound.
A program may use at most 128 MiB of HBM per device.

```python
import jax
import jax.numpy as jnp
from jax import lax

D = 4096
FF = 16384
BLK = 128
TOKENS = 2048
ROW_BLOCKS = 32
COL_BLOCKS = 4
TILES_DEV = 16
N_TP = 32


def tile_cells(key, salt):

    def one_group(sub_key):
        return jax.random.permutation(sub_key, ROW_BLOCKS * COL_BLOCKS)[:TILES_DEV]
    keys = jax.random.split(jax.random.fold_in(key, salt), N_TP)
    return jax.vmap(one_group)(keys).astype(jnp.int32)


def draw_in_rows(key, part):
    return tile_cells(key, 11) // COL_BLOCKS


def draw_in_cols(key, part):
    return tile_cells(key, 11) % COL_BLOCKS


def draw_down_rows(key, part):
    return tile_cells(key, 23) % COL_BLOCKS


def draw_down_cols(key, part):
    return tile_cells(key, 23) // COL_BLOCKS


def shard_levels(rng, dims, cuts, least, high):
    gain, own = 1.0, jax.random.fold_in(rng, 6)
    for axis_at, blocks in cuts:
        heights = jnp.exp(jax.random.uniform(jax.random.fold_in(own, axis_at), (blocks,), jnp.float32, least / len(cuts), high / len(cuts)))
        gain = gain * jnp.repeat(heights, dims[axis_at] // blocks).reshape([-1 if axis == axis_at else 1 for axis in range(len(dims))])
    return gain


def normal_values(stream_key, dims, spread, bound, cuts=(), held_as=jnp.bfloat16):
    entries = jax.random.normal(stream_key, dims, jnp.float32) * spread
    if len(cuts) > 0:
        entries = shard_levels(stream_key, dims, cuts, -0.22, 0.18) * entries
    return jnp.clip(entries, min=-bound, max=bound).astype(held_as)


def setup_inputs(seed: int = 0) -> dict:
    arg_keys = jax.random.split(jax.random.key(seed), 10)
    return {
        "inputs": normal_values(arg_keys[0], (TOKENS, D), 1.0, 6.0, ((0, 4),)),
        "out_grad": normal_values(arg_keys[1], (TOKENS, D), 1.0, 6.0, ((0, 4),)),
        "gate_tiles": normal_values(arg_keys[2], (N_TP, TILES_DEV, BLK, BLK), (D // 8) ** -0.5, 0.25, ((0, 32), (1, 4))),
        "up_tiles": normal_values(arg_keys[3], (N_TP, TILES_DEV, BLK, BLK), (D // 8) ** -0.5, 0.25, ((0, 32), (1, 4))),
        "down_tiles": normal_values(arg_keys[4], (N_TP, TILES_DEV, BLK, BLK), (FF // 8) ** -0.5, 0.125, ((0, 32), (1, 4))),
        "in_rows": draw_in_rows(jax.random.fold_in(arg_keys[9], 71), 0),
        "in_cols": draw_in_cols(jax.random.fold_in(arg_keys[9], 71), 0),
        "down_rows": draw_down_rows(jax.random.fold_in(arg_keys[9], 71), 0),
        "down_cols": draw_down_cols(jax.random.fold_in(arg_keys[9], 71), 0),
    }


def tile_apply(blocks, tiles, rows, cols, count):
    picked = jnp.take(blocks, rows, axis=1).astype(jnp.float32)
    product = jnp.einsum('tkb,kbc->tkc', picked, tiles.astype(jnp.float32), precision=lax.Precision.HIGHEST)
    select = (cols[:, None] == jnp.arange(count, dtype=jnp.int32)[None, :]).astype(jnp.float32)
    return jnp.einsum('tkc,kj->tjc', product, select, precision=lax.Precision.HIGHEST)

def tile_back(blocks, tiles, rows, cols, count):
    picked = jnp.take(blocks, cols, axis=1).astype(jnp.float32)
    product = jnp.einsum('tkc,kbc->tkb', picked, tiles.astype(jnp.float32), precision=lax.Precision.HIGHEST)
    select = (rows[:, None] == jnp.arange(count, dtype=jnp.int32)[None, :]).astype(jnp.float32)
    return jnp.einsum('tkb,kj->tjb', product, select, precision=lax.Precision.HIGHEST)

def tile_grad(left, right, rows, cols):
    picked_left = jnp.take(left, rows, axis=1).astype(jnp.float32)
    picked_right = jnp.take(right, cols, axis=1).astype(jnp.float32)
    return jnp.einsum('tkb,tkc->kbc', picked_left, picked_right, precision=lax.Precision.HIGHEST)

def rounded(value):
    return lax.optimization_barrier(value.astype(jnp.bfloat16)).astype(jnp.float32)

def reference(inputs, out_grad, gate_tiles, up_tiles, down_tiles, in_rows, in_cols, down_rows, down_cols):
    tok_rows = inputs.shape[0]
    in_blocks = inputs.reshape(tok_rows, ROW_BLOCKS, BLK)
    grad_blocks = out_grad.reshape(tok_rows, ROW_BLOCKS, BLK)

    def group(carry, pieces):
        out_total, in_total = carry
        gate_part, up_part, down_part, rows_in, cols_in, rows_dn, cols_dn = pieces
        gate_val = tile_apply(in_blocks, gate_part, rows_in, cols_in, COL_BLOCKS)
        up_val = tile_apply(in_blocks, up_part, rows_in, cols_in, COL_BLOCKS)
        sigmoid_gate = jax.nn.sigmoid(gate_val)
        swish = gate_val * sigmoid_gate
        act = (swish * up_val).astype(jnp.bfloat16)
        partial_out = tile_apply(act, down_part, rows_dn, cols_dn, ROW_BLOCKS)
        act_grad = tile_back(grad_blocks, down_part, rows_dn, cols_dn, COL_BLOCKS)
        gate_back = (act_grad * up_val * sigmoid_gate * (1.0 + gate_val * (1.0 - sigmoid_gate))).astype(jnp.bfloat16)
        up_back = (act_grad * swish).astype(jnp.bfloat16)
        partial_in = tile_back(gate_back, gate_part, rows_in, cols_in, ROW_BLOCKS) + tile_back(up_back, up_part, rows_in, cols_in, ROW_BLOCKS)
        grads = (tile_grad(in_blocks, gate_back, rows_in, cols_in), tile_grad(in_blocks, up_back, rows_in, cols_in), tile_grad(act, grad_blocks, rows_dn, cols_dn))
        return ((out_total + rounded(partial_out), in_total + rounded(partial_in)), grads)
    zeros = jnp.zeros((tok_rows, ROW_BLOCKS, BLK), jnp.float32)
    carry, grads = lax.scan(group, (zeros, zeros), (gate_tiles, up_tiles, down_tiles, in_rows, in_cols, down_rows, down_cols))
    ffn_out = carry[0].astype(jnp.bfloat16).reshape(tok_rows, D)
    input_grad = carry[1].astype(jnp.bfloat16).reshape(tok_rows, D)
    return (ffn_out, input_grad, grads[0], grads[1], grads[2])
```

```python
import functools

import jax
import jax.numpy as jnp
from jax import lax
from jax.experimental import pallas as pl
from jax.experimental.pallas import tpu as pltpu
from jax.sharding import PartitionSpec as P

RING = 4
CHUNKS = 2
F32 = jnp.float32
BF16 = jnp.bfloat16
NT = (((1,), (1,)), ((), ()))
TN = (((0,), (0,)), ((), ()))


def up32(ref, *idx):
    return ref[idx].astype(F32)


def kernel(
    x_hbm, og_hbm, gt_hbm, ut_hbm, dt_hbm, rows_in, cols_in, rows_dn, cols_dn, inv,
    ffn_ref, ing_ref, gg_ref, ug_ref, dg_ref,
    x, og, tg, tu, td, wgu, wd, hid, act, gb, part, rc, r1r, r1f, q2, r2r, r2f, gr, rzr, rzf,
    lsem, ags, agr, cs, cr, s1s, s1r, s2s, s2r, zs, zr,
):
    z = lax.axis_index("fsdp")
    t = lax.axis_index("tp")
    core = lax.rem(t, 2)
    chip = t // 2
    px = lax.rem(chip, RING)
    py = chip // RING
    tok = x.shape[1]
    blk = tg.shape[1]
    n_tiles = tg.shape[0] - 1
    row_blocks = x.shape[0]
    col_blocks = wd.shape[0] // blk
    per = n_tiles // RING
    ct = tok // CHUNKS
    ht = ct // 4

    def wrap(v):
        return lax.rem(v + RING, RING)

    def dev(zz, yy, xx, cc):
        return (zz, (yy * RING + xx) * 2 + cc)

    def nbr(axis, step):
        if axis == "x":
            return dev(z, py, wrap(px + step), core)
        if axis == "y":
            return dev(z, wrap(py + step), px, core)
        return dev(wrap(z + step), py, px, core)

    partner = dev(z, py, px, 1 - core)
    pos = {"x": px, "y": py, "z": z}
    axes = (("x", "y"), ("y", "x"))

    def remote(src, dst, ss, rs, to):
        return pltpu.make_async_remote_copy(
            src_ref=src, dst_ref=dst, send_sem=ss, recv_sem=rs,
            device_id=to, device_id_type=pl.DeviceIdType.MESH,
        )

    sends = []

    def send(src, dst, ss, rs, to):
        c = remote(src, dst, ss, rs, to)
        c.start()
        sends.append(c)

    tiles_hbm = (gt_hbm, ut_hbm, dt_hbm)
    tiles = (tg, tu, td)
    own = pl.ds(z * per, per)
    loads = [
        pltpu.make_async_copy(tiles_hbm[m].at[0], tiles[m].at[own], lsem.at[m]) for m in range(3)
    ]
    for c in loads:
        c.start()

    def load_block(r, carry):
        cols = pl.ds(r * blk, blk)
        pltpu.make_async_copy(x_hbm.at[:, cols], x.at[r], lsem.at[3]).start()
        pltpu.make_async_copy(og_hbm.at[:, cols], og.at[r], lsem.at[4]).start()
        return carry

    lax.fori_loop(0, row_blocks, load_block, 0)

    barrier = pltpu.get_barrier_semaphore()
    everyone = [partner] + [nbr(a, s) for a in "xyz" for s in (1, -1)]
    for to in everyone:
        pl.semaphore_signal(barrier, inc=1, device_id=to, device_id_type=pl.DeviceIdType.MESH)
    pl.semaphore_wait(barrier, len(everyone))

    def ag_own(m):
        for d, step in enumerate((1, -1)):
            send(tiles_hbm[m].at[0], tiles[m].at[own], ags.at[m, d], agr.at[m, d], nbr("z", step))

    def ag_wait(m, d):
        slot = tiles[m].at[pl.ds(wrap(z - 1 if d == 0 else z + 1) * per, per)]
        remote(slot, slot, ags.at[m, d], agr.at[m, d], partner).wait_recv()

    half = per // 2

    def ag_relay(m):
        for d, step in enumerate((1, -1)):
            ag_wait(m, d)
            piece = tiles[m].at[pl.ds(wrap(z - step) * per + d * half, half)]
            send(piece, piece, ags.at[m, 2 + d], agr.at[m, 2 + d], nbr("z", step))

    def ag_last(m):
        for d in range(2):
            piece = tiles[m].at[pl.ds(wrap(z + 2) * per + d * half, half)]
            remote(piece, piece, ags.at[m, 2 + d], agr.at[m, 2 + d], partner).wait_recv()

    ag_own(0)
    ag_own(1)

    for m in range(3):
        tiles[m][n_tiles] = jnp.zeros((blk, blk), BF16)

    ag_relay(0)
    ag_relay(1)
    ag_own(2)
    loads[0].wait()
    loads[1].wait()
    ag_last(0)
    ag_last(1)

    def build_gu(r, carry):
        rows = pl.ds(r * blk, blk)
        for c in range(col_blocks):
            i = inv[0, r * col_blocks + c]
            wgu[rows, 2 * c * blk:(2 * c + 1) * blk] = tg[i]
            wgu[rows, (2 * c + 1) * blk:(2 * c + 2) * blk] = tu[i]
        return carry

    lax.fori_loop(0, row_blocks, build_gu, 0)
    ag_relay(2)
    pltpu.make_async_copy(x, x, lsem.at[3]).wait()

    def wide(ref, rows):
        return jnp.concatenate([ref[r, rows] for r in range(ref.shape[0])], axis=1)

    def forward(n, carry):
        rows = pl.ds((n // col_blocks) * ct, ct)
        c = lax.rem(n, col_blocks)
        cols = pl.ds(c * 2 * blk, 2 * blk)
        h = jnp.dot(wide(x, rows), wgu[:, cols], preferred_element_type=F32)
        hid[rows, cols] = h
        gate = h[:, :blk]
        act[c, rows] = (gate * jax.nn.sigmoid(gate) * h[:, blk:]).astype(BF16)
        return carry

    lax.fori_loop(0, CHUNKS * col_blocks, forward, 0)
    loads[2].wait()
    pltpu.make_async_copy(og, og, lsem.at[4]).wait()
    ag_last(2)

    def build_dn(j, carry):
        cols = pl.ds(j * blk, blk)
        for c in range(col_blocks):
            wd[c * blk:(c + 1) * blk, cols] = td[inv[1, c * row_blocks + j]]
        return carry

    lax.fori_loop(0, row_blocks, build_dn, 0)

    def put(i, n, val):
        yy = n // RING
        xx = lax.rem(n, RING)
        for cc in range(2):
            for a, (d1, d2) in enumerate(((xx, yy), (yy, xx))):
                for h in range(2):
                    r0 = (a * 2 + h) * ht
                    part[i, cc, a, d1, h, d2] = val[r0:r0 + ht, cc * blk:(cc + 1) * blk].astype(BF16)

    def out_part(k):
        def step(n, carry):
            val = jnp.dot(
                wide(act, pl.ds(k * ct, ct)), wd[:, pl.ds(n * 2 * blk, 2 * blk)],
                preferred_element_type=F32,
            )
            put(k, n, val)
            return carry

        lax.fori_loop(0, row_blocks // 2, step, 0)

    def in_part(k):
        def step(n, carry):
            val = lax.dot_general(
                wide(gb, pl.ds(k * ct, ct)), wgu[pl.ds(n * 2 * blk, 2 * blk), :], NT,
                preferred_element_type=F32,
            )
            put(CHUNKS + k, n, val)
            return carry

        lax.fori_loop(0, row_blocks // 2, step, 0)

    def core_send(i):
        for a in range(2):
            send(part.at[i, 1 - core, a], rc.at[i, a], cs.at[i, a], cr.at[i, a], partner)

    def recv(ref, ss, rs):
        remote(ref, ref, ss, rs, partner).wait_recv()

    def ev_a(i):
        for a in range(2):
            ax = axes[a][0]
            p = pos[ax]
            e = i * 2 + a
            recv(rc.at[i, a], cs.at[i, a], cr.at[i, a])
            far = wrap(p + 2)
            part[i, core, a, far] = (up32(part, i, core, a, far) + up32(rc, i, a, far)).astype(BF16)
            for d, s in enumerate((1, -1)):
                send(part.at[i, core, a, far, d], r1r.at[e, d], s1s.at[e, d], s1r.at[e, d], nbr(ax, s))
            for d, s in enumerate((1, -1)):
                q = wrap(p + s)
                h = 1 - d
                part[i, core, a, q, h] = (
                    up32(part, i, core, a, q, h) + up32(rc, i, a, q, h)
                ).astype(BF16)
                send(
                    part.at[i, core, a, q, h], r1f.at[e, d, h], s1s.at[e, 2 + d],
                    s1r.at[e, 2 + d], nbr(ax, s),
                )

    def ev_b(i):
        for a in range(2):
            ax = axes[a][0]
            p = pos[ax]
            e = i * 2 + a
            for d, s in enumerate((1, -1)):
                q = wrap(p + s)
                recv(r1r.at[e, d], s1s.at[e, d], s1r.at[e, d])
                part[i, core, a, q, d] = (
                    up32(part, i, core, a, q, d) + up32(rc, i, a, q, d) + up32(r1r, e, d)
                ).astype(BF16)
                send(
                    part.at[i, core, a, q, d], r1f.at[e, d, d], s1s.at[e, 4 + d],
                    s1r.at[e, 4 + d], nbr(ax, s),
                )

    def ev_c(i):
        for a in range(2):
            ax, ax2 = axes[a]
            p = pos[ax]
            q = pos[ax2]
            e = i * 2 + a
            for d in range(2):
                recv(r1f.at[e, d, 1 - d], s1s.at[e, 2 + d], s1r.at[e, 2 + d])
                recv(r1f.at[e, d, d], s1s.at[e, 4 + d], s1r.at[e, 4 + d])
            for h in range(2):
                val = (
                    up32(part, i, core, a, p, h) + up32(rc, i, a, p, h)
                    + up32(r1f, e, 0, h) + up32(r1f, e, 1, h)
                ).astype(BF16)
                for d2 in range(RING):
                    q2[e, d2, h] = val[d2]
            far = wrap(q + 2)
            for d, s in enumerate((1, -1)):
                send(q2.at[e, far, d], r2r.at[e, d], s2s.at[e, d], s2r.at[e, d], nbr(ax2, s))
            for d, s in enumerate((1, -1)):
                send(
                    q2.at[e, wrap(q + s), 1 - d], r2f.at[e, d, 1 - d], s2s.at[e, 2 + d],
                    s2r.at[e, 2 + d], nbr(ax2, s),
                )

    def ev_d(i):
        for a in range(2):
            ax2 = axes[a][1]
            q = pos[ax2]
            e = i * 2 + a
            for d, s in enumerate((1, -1)):
                w = wrap(q + s)
                recv(r2r.at[e, d], s2s.at[e, d], s2r.at[e, d])
                q2[e, w, d] = (up32(q2, e, w, d) + up32(r2r, e, d)).astype(BF16)
                send(
                    q2.at[e, w, d], r2f.at[e, d, d], s2s.at[e, 4 + d], s2r.at[e, 4 + d],
                    nbr(ax2, s),
                )

    def ev_e(i):
        out = ffn_ref if i < CHUNKS else ing_ref
        for a in range(2):
            q = pos[axes[a][1]]
            e = i * 2 + a
            for d in range(2):
                recv(r2f.at[e, d, 1 - d], s2s.at[e, 2 + d], s2r.at[e, 2 + d])
                recv(r2f.at[e, d, d], s2s.at[e, 4 + d], s2r.at[e, 4 + d])
            for h in range(2):
                r0 = (i % CHUNKS) * ct + (a * 2 + h) * ht
                out[r0:r0 + ht, :] = (
                    up32(q2, e, q, h) + up32(r2f, e, 0, h) + up32(r2f, e, 1, h)
                ).astype(BF16)

    def ev_z0():
        far = wrap(z + 2)
        for d, s in enumerate((1, -1)):
            send(gr.at[far, d], rzr.at[d], zs.at[d], zr.at[d], nbr("z", s))
        for d, s in enumerate((1, -1)):
            send(gr.at[wrap(z + s), 1 - d], rzf.at[d, 1 - d], zs.at[2 + d], zr.at[2 + d], nbr("z", s))

    def ev_z1():
        for d, s in enumerate((1, -1)):
            q = wrap(z + s)
            recv(rzr.at[d], zs.at[d], zr.at[d])
            gr[q, d] = (up32(gr, q, d) + up32(rzr, d)).astype(BF16)
            send(gr.at[q, d], rzf.at[d, d], zs.at[4 + d], zr.at[4 + d], nbr("z", s))

    def ev_z2():
        for d in range(2):
            recv(rzf.at[d, 1 - d], zs.at[2 + d], zr.at[2 + d])
            recv(rzf.at[d, d], zs.at[4 + d], zr.at[4 + d])
        for h in range(2):
            for m, out in enumerate((gg_ref, ug_ref, dg_ref)):
                for e in range(half):
                    out[0, h * half + e] = (
                        up32(gr, z, h, m, e) + up32(rzf, 0, h, m, e) + up32(rzf, 1, h, m, e)
                    )

    def back(k):
        rows = pl.ds(k * ct, ct)

        def step(n, carry):
            ag = lax.dot_general(
                wide(og, rows), wd[pl.ds(n * 2 * blk, 2 * blk), :], NT, preferred_element_type=F32
            )
            for e in range(2):
                c = n * 2 + e
                c0 = c * 2 * blk
                gate = hid[rows, pl.ds(c0, blk)]
                up = hid[rows, pl.ds(c0 + blk, blk)]
                a = ag[:, e * blk:(e + 1) * blk]
                s = jax.nn.sigmoid(gate)
                gb[c, rows, :blk] = (a * up * s * (1.0 + gate * (1.0 - s))).astype(BF16)
                gb[c, rows, blk:] = (a * (gate * s)).astype(BF16)
            return carry

        lax.fori_loop(0, col_blocks // 2, step, 0)

    def grads():
        def step(k, carry):
            d = k // per
            e = lax.rem(k, per)
            h = e // half
            e = lax.rem(e, half)
            xk = x[rows_in[0, k]]
            bk = gb[cols_in[0, k]]
            g = lax.dot_general(xk, bk, TN, preferred_element_type=F32).astype(BF16)
            gr[d, h, 0, e] = g[:, :blk]
            gr[d, h, 1, e] = g[:, blk:]
            ak = act[rows_dn[0, k]]
            ok = og[cols_dn[0, k]]
            gr[d, h, 2, e] = lax.dot_general(ak, ok, TN, preferred_element_type=F32).astype(BF16)
            return carry

        lax.fori_loop(0, n_tiles, step, 0)

    out_part(0)
    core_send(0)
    out_part(1)
    core_send(1)
    ev_a(0)
    back(0)
    ev_a(1)
    ev_b(0)
    back(1)
    ev_b(1)
    in_part(0)
    core_send(2)
    ev_c(0)
    in_part(1)
    core_send(3)
    ev_a(2)
    ev_c(1)
    ev_d(0)
    grads()
    ev_z0()
    ev_a(3)
    ev_b(2)
    ev_e(0)
    ev_d(1)
    ev_b(3)
    ev_c(2)
    ev_z1()
    ev_e(1)
    ev_c(3)
    ev_d(2)
    ev_d(3)
    ev_e(2)
    ev_z2()
    ev_e(3)
    for c in sends:
        c.wait_send()


def on_device(
    inputs, out_grad, gate_tiles, up_tiles, down_tiles, in_rows, in_cols, down_rows, down_cols
):
    tok, width = inputs.shape
    blk = gate_tiles.shape[2]
    n_tiles = in_rows.shape[1]
    row_blocks = width // blk
    hidden = n_tiles * blk // 4
    steps = 2 * CHUNKS
    ht = tok // (CHUNKS * 4)
    half = n_tiles // RING // 2
    ev = steps * 2
    any_spec = pl.BlockSpec(memory_space=pl.ANY)
    smem = pl.BlockSpec(memory_space=pltpu.SMEM)
    vmem = pl.BlockSpec(memory_space=pltpu.VMEM)
    dma = pltpu.SemaphoreType.DMA
    col_blocks = hidden // blk
    keys = jnp.concatenate(
        [in_rows * col_blocks + in_cols, down_rows * row_blocks + down_cols], axis=0
    )
    cells = jnp.arange(row_blocks * col_blocks, dtype=jnp.int32)
    order = jnp.arange(n_tiles, dtype=jnp.int32)
    inv = n_tiles + jnp.sum(
        jnp.where(keys[:, :, None] == cells, order[:, None] - n_tiles, 0), axis=1, dtype=jnp.int32
    )
    return pl.pallas_call(
        kernel,
        out_shape=(
            jax.ShapeDtypeStruct((tok, blk), BF16),
            jax.ShapeDtypeStruct((tok, blk), BF16),
            jax.ShapeDtypeStruct(gate_tiles.shape, F32),
            jax.ShapeDtypeStruct(gate_tiles.shape, F32),
            jax.ShapeDtypeStruct(gate_tiles.shape, F32),
        ),
        in_specs=[any_spec] * 5 + [smem] * 5,
        out_specs=[vmem] * 5,
        scratch_shapes=[
            pltpu.VMEM((row_blocks, tok, blk), BF16),
            pltpu.VMEM((row_blocks, tok, blk), BF16),
            pltpu.VMEM((n_tiles + 1, blk, blk), BF16),
            pltpu.VMEM((n_tiles + 1, blk, blk), BF16),
            pltpu.VMEM((n_tiles + 1, blk, blk), BF16),
            pltpu.VMEM((width, 2 * hidden), BF16),
            pltpu.VMEM((hidden, width), BF16),
            pltpu.VMEM((tok, 2 * hidden), F32),
            pltpu.VMEM((hidden // blk, tok, blk), BF16),
            pltpu.VMEM((hidden // blk, tok, 2 * blk), BF16),
            pltpu.VMEM((steps, 2, 2, RING, 2, RING, ht, blk), BF16),
            pltpu.VMEM((steps, 2, RING, 2, RING, ht, blk), BF16),
            pltpu.VMEM((ev, 2, RING, ht, blk), BF16),
            pltpu.VMEM((ev, 2, 2, RING, ht, blk), BF16),
            pltpu.VMEM((ev, RING, 2, ht, blk), BF16),
            pltpu.VMEM((ev, 2, ht, blk), BF16),
            pltpu.VMEM((ev, 2, 2, ht, blk), BF16),
            pltpu.VMEM((RING, 2, 3, half, blk, blk), BF16),
            pltpu.VMEM((2, 3, half, blk, blk), BF16),
            pltpu.VMEM((2, 2, 3, half, blk, blk), BF16),
            dma((5,)),
            dma((3, 4)),
            dma((3, 4)),
            dma((steps, 2)),
            dma((steps, 2)),
            dma((ev, 6)),
            dma((ev, 6)),
            dma((ev, 6)),
            dma((ev, 6)),
            dma((6,)),
            dma((6,)),
        ],
        compiler_params=pltpu.CompilerParams(
            collective_id=0, has_side_effects=True, vmem_limit_bytes=60 * 1024 * 1024
        ),
    )(inputs, out_grad, gate_tiles, up_tiles, down_tiles, in_rows, in_cols, down_rows, down_cols,
      inv)


def solution(mesh):
    in_specs = (
        P("fsdp", None),
        P("fsdp", None),
        P("tp", "fsdp", None, None),
        P("tp", "fsdp", None, None),
        P("tp", "fsdp", None, None),
        P("tp", None),
        P("tp", None),
        P("tp", None),
        P("tp", None),
    )
    out_specs = (
        P("fsdp", "tp"),
        P("fsdp", "tp"),
        P("tp", "fsdp", None, None),
        P("tp", "fsdp", None, None),
        P("tp", "fsdp", None, None),
    )
    return jax.shard_map(
        on_device, mesh=mesh, in_specs=in_specs, out_specs=out_specs, check_vma=False
    )
```

```python
import functools

import jax
import jax.numpy as jnp
from jax import lax
from jax.experimental import pallas as pl
from jax.experimental.pallas import tpu as pltpu
from jax.sharding import PartitionSpec as P

RING = 4
CHUNKS = 2
F32 = jnp.float32
BF16 = jnp.bfloat16
NT = (((1,), (1,)), ((), ()))
TN = (((0,), (0,)), ((), ()))


def up32(ref, *idx):
    return ref[idx].astype(F32)


def kernel(
    x_hbm, og_hbm, gt_hbm, ut_hbm, dt_hbm, rows_in_hbm, cols_in_hbm, rows_dn_hbm, cols_dn_hbm,
    out_ref, grad_ref,
    x, og, tg, tu, td, wgu, wd, hid, act, gb, part, rc, r1r, r1f, q2, r2r, r2f, gr, rzr, rzf,
    lists, inv_in, inv_dn,
    lsem, ags, agr, cs, cr, s1s, s1r, s2s, s2r, zs, zr,
):
    z = lax.axis_index("fsdp")
    t = lax.axis_index("tp")
    core = lax.rem(t, 2)
    chip = t // 2
    px = lax.rem(chip, RING)
    py = chip // RING
    tok = x.shape[1]
    blk = tg.shape[1]
    n_tiles = tg.shape[0] - 1
    row_blocks = x.shape[0]
    col_blocks = wd.shape[0] // blk
    per = n_tiles // RING
    ct = tok // CHUNKS
    ht = ct // 4

    def wrap(v):
        return lax.rem(v + RING, RING)

    def dev(zz, yy, xx, cc):
        return (zz, (yy * RING + xx) * 2 + cc)

    def nbr(axis, step):
        if axis == "x":
            return dev(z, py, wrap(px + step), core)
        if axis == "y":
            return dev(z, wrap(py + step), px, core)
        return dev(wrap(z + step), py, px, core)

    partner = dev(z, py, px, 1 - core)
    pos = {"x": px, "y": py, "z": z}
    axes = (("x", "y"), ("y", "x"))

    def remote(src, dst, ss, rs, to):
        return pltpu.make_async_remote_copy(
            src_ref=src, dst_ref=dst, send_sem=ss, recv_sem=rs,
            device_id=to, device_id_type=pl.DeviceIdType.MESH,
        )

    sends = []

    def send(src, dst, ss, rs, to):
        c = remote(src, dst, ss, rs, to)
        c.start()
        sends.append(c)

    tiles_hbm = (gt_hbm, ut_hbm, dt_hbm)
    tiles = (tg, tu, td)
    own = pl.ds(z * per, per)
    loads = [
        pltpu.make_async_copy(tiles_hbm[m].at[0], tiles[m].at[own], lsem.at[m]) for m in range(3)
    ]
    for c in loads:
        c.start()

    def load_block(r, carry):
        cols = pl.ds(r * blk, blk)
        pltpu.make_async_copy(x_hbm.at[:, cols], x.at[r], lsem.at[3]).start()
        pltpu.make_async_copy(og_hbm.at[:, cols], og.at[r], lsem.at[4]).start()
        return carry

    lax.fori_loop(0, row_blocks, load_block, 0)

    lists_hbm = (rows_in_hbm, cols_in_hbm, rows_dn_hbm, cols_dn_hbm)
    list_loads = [
        pltpu.make_async_copy(lists_hbm[j].at[0], lists.at[j], lsem.at[5 + j]) for j in range(4)
    ]
    for c in list_loads:
        c.start()

    barrier = pltpu.get_barrier_semaphore()
    everyone = [partner] + [nbr(a, s) for a in "xyz" for s in (1, -1)]
    for to in everyone:
        pl.semaphore_signal(barrier, inc=1, device_id=to, device_id_type=pl.DeviceIdType.MESH)
    pl.semaphore_wait(barrier, len(everyone))

    def ag_own(m):
        for d, step in enumerate((1, -1)):
            send(tiles_hbm[m].at[0], tiles[m].at[own], ags.at[m, d], agr.at[m, d], nbr("z", step))

    def ag_wait(m, d):
        slot = tiles[m].at[pl.ds(wrap(z - 1 if d == 0 else z + 1) * per, per)]
        remote(slot, slot, ags.at[m, d], agr.at[m, d], partner).wait_recv()

    half = per // 2

    def ag_relay(m):
        for d, step in enumerate((1, -1)):
            ag_wait(m, d)
            piece = tiles[m].at[pl.ds(wrap(z - step) * per + d * half, half)]
            send(piece, piece, ags.at[m, 2 + d], agr.at[m, 2 + d], nbr("z", step))

    def ag_last(m):
        for d in range(2):
            piece = tiles[m].at[pl.ds(wrap(z + 2) * per + d * half, half)]
            remote(piece, piece, ags.at[m, 2 + d], agr.at[m, 2 + d], partner).wait_recv()

    ag_own(0)
    ag_own(1)

    for c in list_loads:
        c.wait()
    keys_in = [lists[0, k] * col_blocks + lists[1, k] for k in range(n_tiles)]
    keys_dn = [lists[2, k] * row_blocks + lists[3, k] for k in range(n_tiles)]

    def table(i, carry):
        v = jnp.int32(n_tiles)
        w = jnp.int32(n_tiles)
        for k in range(n_tiles):
            v = jnp.where(keys_in[k] == i, jnp.int32(k), v)
            w = jnp.where(keys_dn[k] == i, jnp.int32(k), w)
        inv_in[i] = v
        inv_dn[i] = w
        return carry

    lax.fori_loop(0, row_blocks * col_blocks, table, 0)
    for m in range(3):
        tiles[m][n_tiles] = jnp.zeros((blk, blk), BF16)

    ag_relay(0)
    ag_relay(1)
    ag_own(2)
    loads[0].wait()
    loads[1].wait()
    ag_last(0)
    ag_last(1)

    def build_gu(r, carry):
        rows = pl.ds(r * blk, blk)
        for c in range(col_blocks):
            i = inv_in[r * col_blocks + c]
            wgu[rows, 2 * c * blk:(2 * c + 1) * blk] = tg[i]
            wgu[rows, (2 * c + 1) * blk:(2 * c + 2) * blk] = tu[i]
        return carry

    lax.fori_loop(0, row_blocks, build_gu, 0)
    ag_relay(2)
    pltpu.make_async_copy(x, x, lsem.at[3]).wait()

    def wide(ref, rows):
        return jnp.concatenate([ref[r, rows] for r in range(ref.shape[0])], axis=1)

    def forward(n, carry):
        rows = pl.ds((n // col_blocks) * ct, ct)
        c = lax.rem(n, col_blocks)
        cols = pl.ds(c * 2 * blk, 2 * blk)
        h = jnp.dot(wide(x, rows), wgu[:, cols], preferred_element_type=F32)
        hid[rows, cols] = h
        gate = h[:, :blk]
        act[c, rows] = (gate * jax.nn.sigmoid(gate) * h[:, blk:]).astype(BF16)
        return carry

    lax.fori_loop(0, CHUNKS * col_blocks, forward, 0)
    loads[2].wait()
    pltpu.make_async_copy(og, og, lsem.at[4]).wait()
    ag_last(2)

    def build_dn(j, carry):
        cols = pl.ds(j * blk, blk)
        for c in range(col_blocks):
            wd[c * blk:(c + 1) * blk, cols] = td[inv_dn[c * row_blocks + j]]
        return carry

    lax.fori_loop(0, row_blocks, build_dn, 0)

    def put(i, n, val):
        yy = n // RING
        xx = lax.rem(n, RING)
        for cc in range(2):
            for a, (d1, d2) in enumerate(((xx, yy), (yy, xx))):
                for h in range(2):
                    r0 = (a * 2 + h) * ht
                    part[i, cc, a, d1, h, d2] = val[r0:r0 + ht, cc * blk:(cc + 1) * blk].astype(BF16)

    def out_part(k):
        def step(n, carry):
            val = jnp.dot(
                wide(act, pl.ds(k * ct, ct)), wd[:, pl.ds(n * 2 * blk, 2 * blk)],
                preferred_element_type=F32,
            )
            put(k, n, val)
            return carry

        lax.fori_loop(0, row_blocks // 2, step, 0)

    def in_part(k):
        def step(n, carry):
            val = lax.dot_general(
                wide(gb, pl.ds(k * ct, ct)), wgu[pl.ds(n * 2 * blk, 2 * blk), :], NT,
                preferred_element_type=F32,
            )
            put(CHUNKS + k, n, val)
            return carry

        lax.fori_loop(0, row_blocks // 2, step, 0)

    def core_send(i):
        for a in range(2):
            send(part.at[i, 1 - core, a], rc.at[i, a], cs.at[i, a], cr.at[i, a], partner)

    def recv(ref, ss, rs):
        remote(ref, ref, ss, rs, partner).wait_recv()

    def ev_a(i):
        for a in range(2):
            ax = axes[a][0]
            p = pos[ax]
            e = i * 2 + a
            recv(rc.at[i, a], cs.at[i, a], cr.at[i, a])
            far = wrap(p + 2)
            part[i, core, a, far] = (up32(part, i, core, a, far) + up32(rc, i, a, far)).astype(BF16)
            for d, s in enumerate((1, -1)):
                send(part.at[i, core, a, far, d], r1r.at[e, d], s1s.at[e, d], s1r.at[e, d], nbr(ax, s))
            for d, s in enumerate((1, -1)):
                q = wrap(p + s)
                h = 1 - d
                part[i, core, a, q, h] = (
                    up32(part, i, core, a, q, h) + up32(rc, i, a, q, h)
                ).astype(BF16)
                send(
                    part.at[i, core, a, q, h], r1f.at[e, d, h], s1s.at[e, 2 + d],
                    s1r.at[e, 2 + d], nbr(ax, s),
                )

    def ev_b(i):
        for a in range(2):
            ax = axes[a][0]
            p = pos[ax]
            e = i * 2 + a
            for d, s in enumerate((1, -1)):
                q = wrap(p + s)
                recv(r1r.at[e, d], s1s.at[e, d], s1r.at[e, d])
                part[i, core, a, q, d] = (
                    up32(part, i, core, a, q, d) + up32(rc, i, a, q, d) + up32(r1r, e, d)
                ).astype(BF16)
                send(
                    part.at[i, core, a, q, d], r1f.at[e, d, d], s1s.at[e, 4 + d],
                    s1r.at[e, 4 + d], nbr(ax, s),
                )

    def ev_c(i):
        for a in range(2):
            ax, ax2 = axes[a]
            p = pos[ax]
            q = pos[ax2]
            e = i * 2 + a
            for d in range(2):
                recv(r1f.at[e, d, 1 - d], s1s.at[e, 2 + d], s1r.at[e, 2 + d])
                recv(r1f.at[e, d, d], s1s.at[e, 4 + d], s1r.at[e, 4 + d])
            for h in range(2):
                val = (
                    up32(part, i, core, a, p, h) + up32(rc, i, a, p, h)
                    + up32(r1f, e, 0, h) + up32(r1f, e, 1, h)
                ).astype(BF16)
                for d2 in range(RING):
                    q2[e, d2, h] = val[d2]
            far = wrap(q + 2)
            for d, s in enumerate((1, -1)):
                send(q2.at[e, far, d], r2r.at[e, d], s2s.at[e, d], s2r.at[e, d], nbr(ax2, s))
            for d, s in enumerate((1, -1)):
                send(
                    q2.at[e, wrap(q + s), 1 - d], r2f.at[e, d, 1 - d], s2s.at[e, 2 + d],
                    s2r.at[e, 2 + d], nbr(ax2, s),
                )

    def ev_d(i):
        for a in range(2):
            ax2 = axes[a][1]
            q = pos[ax2]
            e = i * 2 + a
            for d, s in enumerate((1, -1)):
                w = wrap(q + s)
                recv(r2r.at[e, d], s2s.at[e, d], s2r.at[e, d])
                q2[e, w, d] = (up32(q2, e, w, d) + up32(r2r, e, d)).astype(BF16)
                send(
                    q2.at[e, w, d], r2f.at[e, d, d], s2s.at[e, 4 + d], s2r.at[e, 4 + d],
                    nbr(ax2, s),
                )

    def ev_e(i):
        for a in range(2):
            q = pos[axes[a][1]]
            e = i * 2 + a
            for d in range(2):
                recv(r2f.at[e, d, 1 - d], s2s.at[e, 2 + d], s2r.at[e, 2 + d])
                recv(r2f.at[e, d, d], s2s.at[e, 4 + d], s2r.at[e, 4 + d])
            for h in range(2):
                r0 = (i % CHUNKS) * ct + (a * 2 + h) * ht
                out_ref[i // CHUNKS, r0:r0 + ht, :] = (
                    up32(q2, e, q, h) + up32(r2f, e, 0, h) + up32(r2f, e, 1, h)
                ).astype(BF16)

    def ev_z0():
        far = wrap(z + 2)
        for d, s in enumerate((1, -1)):
            send(gr.at[far, d], rzr.at[d], zs.at[d], zr.at[d], nbr("z", s))
        for d, s in enumerate((1, -1)):
            send(gr.at[wrap(z + s), 1 - d], rzf.at[d, 1 - d], zs.at[2 + d], zr.at[2 + d], nbr("z", s))

    def ev_z1():
        for d, s in enumerate((1, -1)):
            q = wrap(z + s)
            recv(rzr.at[d], zs.at[d], zr.at[d])
            gr[q, d] = (up32(gr, q, d) + up32(rzr, d)).astype(BF16)
            send(gr.at[q, d], rzf.at[d, d], zs.at[4 + d], zr.at[4 + d], nbr("z", s))

    def ev_z2():
        for d in range(2):
            recv(rzf.at[d, 1 - d], zs.at[2 + d], zr.at[2 + d])
            recv(rzf.at[d, d], zs.at[4 + d], zr.at[4 + d])
        for h in range(2):
            for m in range(3):
                for e in range(half):
                    grad_ref[m, h * half + e] = (
                        up32(gr, z, h, m, e) + up32(rzf, 0, h, m, e) + up32(rzf, 1, h, m, e)
                    )

    def back(k):
        rows = pl.ds(k * ct, ct)

        def step(n, carry):
            ag = lax.dot_general(
                wide(og, rows), wd[pl.ds(n * 2 * blk, 2 * blk), :], NT, preferred_element_type=F32
            )
            for e in range(2):
                c = n * 2 + e
                c0 = c * 2 * blk
                gate = hid[rows, pl.ds(c0, blk)]
                up = hid[rows, pl.ds(c0 + blk, blk)]
                a = ag[:, e * blk:(e + 1) * blk]
                s = jax.nn.sigmoid(gate)
                gb[c, rows, :blk] = (a * up * s * (1.0 + gate * (1.0 - s))).astype(BF16)
                gb[c, rows, blk:] = (a * (gate * s)).astype(BF16)
            return carry

        lax.fori_loop(0, col_blocks // 2, step, 0)

    def grads():
        def step(k, carry):
            d = k // per
            e = lax.rem(k, per)
            h = e // half
            e = lax.rem(e, half)
            xk = x[lists[0, k]]
            bk = gb[lists[1, k]]
            g = lax.dot_general(xk, bk, TN, preferred_element_type=F32).astype(BF16)
            gr[d, h, 0, e] = g[:, :blk]
            gr[d, h, 1, e] = g[:, blk:]
            ak = act[lists[2, k]]
            ok = og[lists[3, k]]
            gr[d, h, 2, e] = lax.dot_general(ak, ok, TN, preferred_element_type=F32).astype(BF16)
            return carry

        lax.fori_loop(0, n_tiles, step, 0)

    out_part(0)
    core_send(0)
    out_part(1)
    core_send(1)
    ev_a(0)
    back(0)
    ev_a(1)
    ev_b(0)
    back(1)
    ev_b(1)
    in_part(0)
    core_send(2)
    ev_c(0)
    in_part(1)
    core_send(3)
    ev_a(2)
    ev_c(1)
    ev_d(0)
    grads()
    ev_z0()
    ev_a(3)
    ev_b(2)
    ev_e(0)
    ev_d(1)
    ev_b(3)
    ev_c(2)
    ev_z1()
    ev_e(1)
    ev_c(3)
    ev_d(2)
    ev_d(3)
    ev_e(2)
    ev_z2()
    ev_e(3)
    for c in sends:
        c.wait_send()


def finish(sums, tile_sums, ffn_ref, ing_ref, gg_ref, ug_ref, dg_ref):
    ffn_ref[...] = sums[0]
    ing_ref[...] = sums[1]
    for m, ref in enumerate((gg_ref, ug_ref, dg_ref)):
        ref[0] = tile_sums[m]


def on_device(
    inputs, out_grad, gate_tiles, up_tiles, down_tiles, in_rows, in_cols, down_rows, down_cols
):
    tok, width = inputs.shape
    blk = gate_tiles.shape[2]
    n_tiles = in_rows.shape[1]
    row_blocks = width // blk
    hidden = n_tiles * blk // 4
    steps = 2 * CHUNKS
    ht = tok // (CHUNKS * 4)
    half = n_tiles // RING // 2
    ev = steps * 2
    any_spec = pl.BlockSpec(memory_space=pl.ANY)
    vmem = pl.BlockSpec(memory_space=pltpu.VMEM)
    dma = pltpu.SemaphoreType.DMA
    entries = row_blocks * hidden // blk
    sums, tile_sums = pl.pallas_call(
        kernel,
        out_shape=(
            jax.ShapeDtypeStruct((2, tok, blk), BF16),
            jax.ShapeDtypeStruct((3,) + gate_tiles.shape[1:], F32),
        ),
        in_specs=[any_spec] * 9,
        out_specs=[vmem] * 2,
        scratch_shapes=[
            pltpu.VMEM((row_blocks, tok, blk), BF16),
            pltpu.VMEM((row_blocks, tok, blk), BF16),
            pltpu.VMEM((n_tiles + 1, blk, blk), BF16),
            pltpu.VMEM((n_tiles + 1, blk, blk), BF16),
            pltpu.VMEM((n_tiles + 1, blk, blk), BF16),
            pltpu.VMEM((width, 2 * hidden), BF16),
            pltpu.VMEM((hidden, width), BF16),
            pltpu.VMEM((tok, 2 * hidden), F32),
            pltpu.VMEM((hidden // blk, tok, blk), BF16),
            pltpu.VMEM((hidden // blk, tok, 2 * blk), BF16),
            pltpu.VMEM((steps, 2, 2, RING, 2, RING, ht, blk), BF16),
            pltpu.VMEM((steps, 2, RING, 2, RING, ht, blk), BF16),
            pltpu.VMEM((ev, 2, RING, ht, blk), BF16),
            pltpu.VMEM((ev, 2, 2, RING, ht, blk), BF16),
            pltpu.VMEM((ev, RING, 2, ht, blk), BF16),
            pltpu.VMEM((ev, 2, ht, blk), BF16),
            pltpu.VMEM((ev, 2, 2, ht, blk), BF16),
            pltpu.VMEM((RING, 2, 3, half, blk, blk), BF16),
            pltpu.VMEM((2, 3, half, blk, blk), BF16),
            pltpu.VMEM((2, 2, 3, half, blk, blk), BF16),
            pltpu.SMEM((4, n_tiles), jnp.int32),
            pltpu.SMEM((entries,), jnp.int32),
            pltpu.SMEM((entries,), jnp.int32),
            dma((9,)),
            dma((3, 4)),
            dma((3, 4)),
            dma((steps, 2)),
            dma((steps, 2)),
            dma((ev, 6)),
            dma((ev, 6)),
            dma((ev, 6)),
            dma((ev, 6)),
            dma((6,)),
            dma((6,)),
        ],
        compiler_params=pltpu.CompilerParams(
            collective_id=0, has_side_effects=True, vmem_limit_bytes=60 * 1024 * 1024
        ),
    )(inputs, out_grad, gate_tiles, up_tiles, down_tiles, in_rows, in_cols, down_rows, down_cols)
    return pl.pallas_call(
        finish,
        out_shape=(jax.ShapeDtypeStruct((tok, blk), BF16),) * 2
        + (jax.ShapeDtypeStruct(gate_tiles.shape, F32),) * 3,
        in_specs=[vmem] * 2,
        out_specs=[vmem] * 5,
    )(sums, tile_sums)


def solution(mesh):
    in_specs = (
        P("fsdp", None),
        P("fsdp", None),
        P("tp", "fsdp", None, None),
        P("tp", "fsdp", None, None),
        P("tp", "fsdp", None, None),
        P("tp", None),
        P("tp", None),
        P("tp", None),
        P("tp", None),
    )
    out_specs = (
        P("fsdp", "tp"),
        P("fsdp", "tp"),
        P("tp", "fsdp", None, None),
        P("tp", "fsdp", None, None),
        P("tp", "fsdp", None, None),
    )
    return jax.shard_map(
        on_device, mesh=mesh, in_specs=in_specs, out_specs=out_specs, check_vma=False
    )
```

```python
import functools

import jax
import jax.numpy as jnp
from jax import lax
from jax.experimental import pallas as pl
from jax.experimental.pallas import tpu as pltpu
from jax.sharding import PartitionSpec as P

RING = 4
CHUNKS = 2
F32 = jnp.float32
BF16 = jnp.bfloat16
NT = (((1,), (1,)), ((), ()))
TN = (((0,), (0,)), ((), ()))


def up32(ref, *idx):
    return ref[idx].astype(F32)


def kernel(
    x_hbm, og_hbm, gt_hbm, ut_hbm, dt_hbm, rows_in_hbm, cols_in_hbm, rows_dn_hbm, cols_dn_hbm,
    out_ref, grad_ref,
    x, og, tg, tu, td, wgu, wd, hid, act, gb, part, rc, r1r, r1f, q2, r2r, r2f, gr, rzr, rzf,
    lists, inv_in, inv_dn,
    lsem, ags, agr, cs, cr, s1s, s1r, s2s, s2r, zs, zr,
):
    z = lax.axis_index("fsdp")
    t = lax.axis_index("tp")
    core = lax.rem(t, 2)
    chip = t // 2
    px = lax.rem(chip, RING)
    py = chip // RING
    tok = x.shape[1]
    blk = tg.shape[1]
    n_tiles = tg.shape[0] - 1
    row_blocks = x.shape[0]
    col_blocks = wd.shape[0] // blk
    per = n_tiles // RING
    ct = tok // CHUNKS
    ht = ct // 4

    def wrap(v):
        return lax.rem(v + RING, RING)

    def dev(zz, yy, xx, cc):
        return (zz, (yy * RING + xx) * 2 + cc)

    def nbr(axis, step):
        if axis == "x":
            return dev(z, py, wrap(px + step), core)
        if axis == "y":
            return dev(z, wrap(py + step), px, core)
        return dev(wrap(z + step), py, px, core)

    partner = dev(z, py, px, 1 - core)
    pos = {"x": px, "y": py, "z": z}
    axes = (("x", "y"), ("y", "x"))

    def remote(src, dst, ss, rs, to):
        return pltpu.make_async_remote_copy(
            src_ref=src, dst_ref=dst, send_sem=ss, recv_sem=rs,
            device_id=to, device_id_type=pl.DeviceIdType.MESH,
        )

    sends = []

    def send(src, dst, ss, rs, to):
        c = remote(src, dst, ss, rs, to)
        c.start()
        sends.append(c)

    tiles_hbm = (gt_hbm, ut_hbm, dt_hbm)
    tiles = (tg, tu, td)
    own = pl.ds(z * per, per)
    loads = [
        pltpu.make_async_copy(tiles_hbm[m].at[0], tiles[m].at[own], lsem.at[m]) for m in range(3)
    ]
    for c in loads:
        c.start()

    def load_block(r, carry):
        cols = pl.ds(r * blk, blk)
        pltpu.make_async_copy(x_hbm.at[:, cols], x.at[r], lsem.at[3]).start()
        pltpu.make_async_copy(og_hbm.at[:, cols], og.at[r], lsem.at[4]).start()
        return carry

    lax.fori_loop(0, row_blocks, load_block, 0)

    lists_hbm = (rows_in_hbm, cols_in_hbm, rows_dn_hbm, cols_dn_hbm)
    list_loads = [
        pltpu.make_async_copy(lists_hbm[j].at[0], lists.at[j], lsem.at[5 + j]) for j in range(4)
    ]
    for c in list_loads:
        c.start()

    barrier = pltpu.get_barrier_semaphore()
    everyone = [partner] + [nbr(a, s) for a in "xyz" for s in (1, -1)]
    for to in everyone:
        pl.semaphore_signal(barrier, inc=1, device_id=to, device_id_type=pl.DeviceIdType.MESH)
    pl.semaphore_wait(barrier, len(everyone))

    def ag_own(m):
        for d, step in enumerate((1, -1)):
            send(tiles_hbm[m].at[0], tiles[m].at[own], ags.at[m, d], agr.at[m, d], nbr("z", step))

    def ag_wait(m, d):
        slot = tiles[m].at[pl.ds(wrap(z - 1 if d == 0 else z + 1) * per, per)]
        remote(slot, slot, ags.at[m, d], agr.at[m, d], partner).wait_recv()

    half = per // 2

    def ag_relay(m):
        for d, step in enumerate((1, -1)):
            ag_wait(m, d)
            piece = tiles[m].at[pl.ds(wrap(z - step) * per + d * half, half)]
            send(piece, piece, ags.at[m, 2 + d], agr.at[m, 2 + d], nbr("z", step))

    def ag_last(m):
        for d in range(2):
            piece = tiles[m].at[pl.ds(wrap(z + 2) * per + d * half, half)]
            remote(piece, piece, ags.at[m, 2 + d], agr.at[m, 2 + d], partner).wait_recv()

    ag_own(0)
    ag_own(1)

    for c in list_loads:
        c.wait()
    keys_in = [lists[0, k] * col_blocks + lists[1, k] for k in range(n_tiles)]
    keys_dn = [lists[2, k] * row_blocks + lists[3, k] for k in range(n_tiles)]

    def table(i, carry):
        v = jnp.int32(n_tiles)
        w = jnp.int32(n_tiles)
        for k in range(n_tiles):
            v = jnp.where(keys_in[k] == i, jnp.int32(k), v)
            w = jnp.where(keys_dn[k] == i, jnp.int32(k), w)
        inv_in[i] = v
        inv_dn[i] = w
        return carry

    lax.fori_loop(0, row_blocks * col_blocks, table, 0)
    for m in range(3):
        tiles[m][n_tiles] = jnp.zeros((blk, blk), BF16)

    ag_relay(0)
    ag_relay(1)
    ag_own(2)
    loads[0].wait()
    loads[1].wait()
    ag_last(0)
    ag_last(1)

    def build_gu(r, carry):
        rows = pl.ds(r * blk, blk)
        for c in range(col_blocks):
            i = inv_in[r * col_blocks + c]
            wgu[rows, 2 * c * blk:(2 * c + 1) * blk] = tg[i]
            wgu[rows, (2 * c + 1) * blk:(2 * c + 2) * blk] = tu[i]
        return carry

    lax.fori_loop(0, row_blocks, build_gu, 0)
    ag_relay(2)
    pltpu.make_async_copy(x, x, lsem.at[3]).wait()

    def wide(ref, rows):
        return jnp.concatenate([ref[r, rows] for r in range(ref.shape[0])], axis=1)

    def forward(n, carry):
        rows = pl.ds((n // col_blocks) * ct, ct)
        c = lax.rem(n, col_blocks)
        cols = pl.ds(c * 2 * blk, 2 * blk)
        h = jnp.dot(wide(x, rows), wgu[:, cols], preferred_element_type=F32)
        hid[rows, cols] = h
        gate = h[:, :blk]
        act[c, rows] = (gate * jax.nn.sigmoid(gate) * h[:, blk:]).astype(BF16)
        return carry

    lax.fori_loop(0, CHUNKS * col_blocks, forward, 0)
    loads[2].wait()
    pltpu.make_async_copy(og, og, lsem.at[4]).wait()
    ag_last(2)

    def build_dn(j, carry):
        cols = pl.ds(j * blk, blk)
        for c in range(col_blocks):
            wd[c * blk:(c + 1) * blk, cols] = td[inv_dn[c * row_blocks + j]]
        return carry

    lax.fori_loop(0, row_blocks, build_dn, 0)

    def put(i, yy, xx, val):
        for cc in range(2):
            for a, (d1, d2) in enumerate(((xx, yy), (yy, xx))):
                for h in range(2):
                    r0 = (a * 2 + h) * ht
                    part[i, cc, a, d1, h, d2] = val[r0:r0 + ht, cc * blk:(cc + 1) * blk].astype(BF16)

    def out_part(k):
        def step(yy, carry):
            lhs = wide(act, pl.ds(k * ct, ct))
            for xx in range(RING):
                cols = pl.ds((yy * RING + xx) * 2 * blk, 2 * blk)
                put(k, yy, xx, jnp.dot(lhs, wd[:, cols], preferred_element_type=F32))
            return carry

        lax.fori_loop(0, RING, step, 0)

    def in_part(k):
        def step(yy, carry):
            lhs = wide(gb, pl.ds(k * ct, ct))
            for xx in range(RING):
                rows = pl.ds((yy * RING + xx) * 2 * blk, 2 * blk)
                put(
                    CHUNKS + k, yy, xx,
                    lax.dot_general(lhs, wgu[rows, :], NT, preferred_element_type=F32),
                )
            return carry

        lax.fori_loop(0, RING, step, 0)

    def core_send(i):
        for a in range(2):
            send(part.at[i, 1 - core, a], rc.at[i, a], cs.at[i, a], cr.at[i, a], partner)

    def recv(ref, ss, rs):
        remote(ref, ref, ss, rs, partner).wait_recv()

    def ev_a(i):
        for a in range(2):
            ax = axes[a][0]
            p = pos[ax]
            e = i * 2 + a
            recv(rc.at[i, a], cs.at[i, a], cr.at[i, a])
            far = wrap(p + 2)
            part[i, core, a, far] = (up32(part, i, core, a, far) + up32(rc, i, a, far)).astype(BF16)
            for d, s in enumerate((1, -1)):
                send(part.at[i, core, a, far, d], r1r.at[e, d], s1s.at[e, d], s1r.at[e, d], nbr(ax, s))
            for d, s in enumerate((1, -1)):
                q = wrap(p + s)
                h = 1 - d
                part[i, core, a, q, h] = (
                    up32(part, i, core, a, q, h) + up32(rc, i, a, q, h)
                ).astype(BF16)
                send(
                    part.at[i, core, a, q, h], r1f.at[e, d, h], s1s.at[e, 2 + d],
                    s1r.at[e, 2 + d], nbr(ax, s),
                )

    def ev_b(i):
        for a in range(2):
            ax = axes[a][0]
            p = pos[ax]
            e = i * 2 + a
            for d, s in enumerate((1, -1)):
                q = wrap(p + s)
                recv(r1r.at[e, d], s1s.at[e, d], s1r.at[e, d])
                part[i, core, a, q, d] = (
                    up32(part, i, core, a, q, d) + up32(rc, i, a, q, d) + up32(r1r, e, d)
                ).astype(BF16)
                send(
                    part.at[i, core, a, q, d], r1f.at[e, d, d], s1s.at[e, 4 + d],
                    s1r.at[e, 4 + d], nbr(ax, s),
                )

    def ev_c(i):
        for a in range(2):
            ax, ax2 = axes[a]
            p = pos[ax]
            q = pos[ax2]
            e = i * 2 + a
            for d in range(2):
                recv(r1f.at[e, d, 1 - d], s1s.at[e, 2 + d], s1r.at[e, 2 + d])
                recv(r1f.at[e, d, d], s1s.at[e, 4 + d], s1r.at[e, 4 + d])
            for h in range(2):
                val = (
                    up32(part, i, core, a, p, h) + up32(rc, i, a, p, h)
                    + up32(r1f, e, 0, h) + up32(r1f, e, 1, h)
                ).astype(BF16)
                for d2 in range(RING):
                    q2[e, d2, h] = val[d2]
            far = wrap(q + 2)
            for d, s in enumerate((1, -1)):
                send(q2.at[e, far, d], r2r.at[e, d], s2s.at[e, d], s2r.at[e, d], nbr(ax2, s))
            for d, s in enumerate((1, -1)):
                send(
                    q2.at[e, wrap(q + s), 1 - d], r2f.at[e, d, 1 - d], s2s.at[e, 2 + d],
                    s2r.at[e, 2 + d], nbr(ax2, s),
                )

    def ev_d(i):
        for a in range(2):
            ax2 = axes[a][1]
            q = pos[ax2]
            e = i * 2 + a
            for d, s in enumerate((1, -1)):
                w = wrap(q + s)
                recv(r2r.at[e, d], s2s.at[e, d], s2r.at[e, d])
                q2[e, w, d] = (up32(q2, e, w, d) + up32(r2r, e, d)).astype(BF16)
                send(
                    q2.at[e, w, d], r2f.at[e, d, d], s2s.at[e, 4 + d], s2r.at[e, 4 + d],
                    nbr(ax2, s),
                )

    def ev_e(i):
        for a in range(2):
            q = pos[axes[a][1]]
            e = i * 2 + a
            for d in range(2):
                recv(r2f.at[e, d, 1 - d], s2s.at[e, 2 + d], s2r.at[e, 2 + d])
                recv(r2f.at[e, d, d], s2s.at[e, 4 + d], s2r.at[e, 4 + d])
            for h in range(2):
                r0 = (i % CHUNKS) * ct + (a * 2 + h) * ht
                out_ref[i // CHUNKS, r0:r0 + ht, :] = (
                    up32(q2, e, q, h) + up32(r2f, e, 0, h) + up32(r2f, e, 1, h)
                ).astype(BF16)

    def ev_z0():
        far = wrap(z + 2)
        for d, s in enumerate((1, -1)):
            send(gr.at[far, d], rzr.at[d], zs.at[d], zr.at[d], nbr("z", s))
        for d, s in enumerate((1, -1)):
            send(gr.at[wrap(z + s), 1 - d], rzf.at[d, 1 - d], zs.at[2 + d], zr.at[2 + d], nbr("z", s))

    def ev_z1():
        for d, s in enumerate((1, -1)):
            q = wrap(z + s)
            recv(rzr.at[d], zs.at[d], zr.at[d])
            gr[q, d] = (up32(gr, q, d) + up32(rzr, d)).astype(BF16)
            send(gr.at[q, d], rzf.at[d, d], zs.at[4 + d], zr.at[4 + d], nbr("z", s))

    def ev_z2():
        for d in range(2):
            recv(rzf.at[d, 1 - d], zs.at[2 + d], zr.at[2 + d])
            recv(rzf.at[d, d], zs.at[4 + d], zr.at[4 + d])
        for h in range(2):
            for m in range(3):
                for e in range(half):
                    grad_ref[m, h * half + e] = (
                        up32(gr, z, h, m, e) + up32(rzf, 0, h, m, e) + up32(rzf, 1, h, m, e)
                    )

    def back(k):
        rows = pl.ds(k * ct, ct)

        def step(n, carry):
            ag = lax.dot_general(
                wide(og, rows), wd[pl.ds(n * 2 * blk, 2 * blk), :], NT, preferred_element_type=F32
            )
            for e in range(2):
                c = n * 2 + e
                c0 = c * 2 * blk
                gate = hid[rows, pl.ds(c0, blk)]
                up = hid[rows, pl.ds(c0 + blk, blk)]
                a = ag[:, e * blk:(e + 1) * blk]
                s = jax.nn.sigmoid(gate)
                gb[c, rows, :blk] = (a * up * s * (1.0 + gate * (1.0 - s))).astype(BF16)
                gb[c, rows, blk:] = (a * (gate * s)).astype(BF16)
            return carry

        lax.fori_loop(0, col_blocks // 2, step, 0)

    def grads():
        def step(k, carry):
            d = k // per
            e = lax.rem(k, per)
            h = e // half
            e = lax.rem(e, half)
            xk = x[lists[0, k]]
            bk = gb[lists[1, k]]
            g = lax.dot_general(xk, bk, TN, preferred_element_type=F32).astype(BF16)
            gr[d, h, 0, e] = g[:, :blk]
            gr[d, h, 1, e] = g[:, blk:]
            ak = act[lists[2, k]]
            ok = og[lists[3, k]]
            gr[d, h, 2, e] = lax.dot_general(ak, ok, TN, preferred_element_type=F32).astype(BF16)
            return carry

        lax.fori_loop(0, n_tiles, step, 0)

    out_part(0)
    core_send(0)
    out_part(1)
    core_send(1)
    ev_a(0)
    back(0)
    ev_a(1)
    ev_b(0)
    back(1)
    in_part(0)
    core_send(2)
    ev_b(1)
    ev_c(0)
    grads()
    ev_z0()
    ev_a(2)
    ev_d(0)
    ev_c(1)
    in_part(1)
    core_send(3)
    ev_b(2)
    ev_e(0)
    ev_a(3)
    ev_d(1)
    ev_z1()
    ev_b(3)
    ev_c(2)
    ev_e(1)
    ev_d(2)
    ev_c(3)
    ev_z2()
    ev_e(2)
    ev_d(3)
    ev_e(3)
    for c in sends:
        c.wait_send()


def finish(sums, tile_sums, ffn_ref, ing_ref, gg_ref, ug_ref, dg_ref):
    ffn_ref[...] = sums[0]
    ing_ref[...] = sums[1]
    for m, ref in enumerate((gg_ref, ug_ref, dg_ref)):
        ref[0] = tile_sums[m]


def on_device(
    inputs, out_grad, gate_tiles, up_tiles, down_tiles, in_rows, in_cols, down_rows, down_cols
):
    tok, width = inputs.shape
    blk = gate_tiles.shape[2]
    n_tiles = in_rows.shape[1]
    row_blocks = width // blk
    hidden = n_tiles * blk // 4
    steps = 2 * CHUNKS
    ht = tok // (CHUNKS * 4)
    half = n_tiles // RING // 2
    ev = steps * 2
    any_spec = pl.BlockSpec(memory_space=pl.ANY)
    vmem = pl.BlockSpec(memory_space=pltpu.VMEM)
    dma = pltpu.SemaphoreType.DMA
    entries = row_blocks * hidden // blk
    sums, tile_sums = pl.pallas_call(
        kernel,
        out_shape=(
            jax.ShapeDtypeStruct((2, tok, blk), BF16),
            jax.ShapeDtypeStruct((3,) + gate_tiles.shape[1:], F32),
        ),
        in_specs=[any_spec] * 9,
        out_specs=[vmem] * 2,
        scratch_shapes=[
            pltpu.VMEM((row_blocks, tok, blk), BF16),
            pltpu.VMEM((row_blocks, tok, blk), BF16),
            pltpu.VMEM((n_tiles + 1, blk, blk), BF16),
            pltpu.VMEM((n_tiles + 1, blk, blk), BF16),
            pltpu.VMEM((n_tiles + 1, blk, blk), BF16),
            pltpu.VMEM((width, 2 * hidden), BF16),
            pltpu.VMEM((hidden, width), BF16),
            pltpu.VMEM((tok, 2 * hidden), F32),
            pltpu.VMEM((hidden // blk, tok, blk), BF16),
            pltpu.VMEM((hidden // blk, tok, 2 * blk), BF16),
            pltpu.VMEM((steps, 2, 2, RING, 2, RING, ht, blk), BF16),
            pltpu.VMEM((steps, 2, RING, 2, RING, ht, blk), BF16),
            pltpu.VMEM((ev, 2, RING, ht, blk), BF16),
            pltpu.VMEM((ev, 2, 2, RING, ht, blk), BF16),
            pltpu.VMEM((ev, RING, 2, ht, blk), BF16),
            pltpu.VMEM((ev, 2, ht, blk), BF16),
            pltpu.VMEM((ev, 2, 2, ht, blk), BF16),
            pltpu.VMEM((RING, 2, 3, half, blk, blk), BF16),
            pltpu.VMEM((2, 3, half, blk, blk), BF16),
            pltpu.VMEM((2, 2, 3, half, blk, blk), BF16),
            pltpu.SMEM((4, n_tiles), jnp.int32),
            pltpu.SMEM((entries,), jnp.int32),
            pltpu.SMEM((entries,), jnp.int32),
            dma((9,)),
            dma((3, 4)),
            dma((3, 4)),
            dma((steps, 2)),
            dma((steps, 2)),
            dma((ev, 6)),
            dma((ev, 6)),
            dma((ev, 6)),
            dma((ev, 6)),
            dma((6,)),
            dma((6,)),
        ],
        compiler_params=pltpu.CompilerParams(
            collective_id=0, has_side_effects=True, vmem_limit_bytes=60 * 1024 * 1024
        ),
    )(inputs, out_grad, gate_tiles, up_tiles, down_tiles, in_rows, in_cols, down_rows, down_cols)
    return pl.pallas_call(
        finish,
        out_shape=(jax.ShapeDtypeStruct((tok, blk), BF16),) * 2
        + (jax.ShapeDtypeStruct(gate_tiles.shape, F32),) * 3,
        in_specs=[vmem] * 2,
        out_specs=[vmem] * 5,
    )(sums, tile_sums)


def solution(mesh):
    in_specs = (
        P("fsdp", None),
        P("fsdp", None),
        P("tp", "fsdp", None, None),
        P("tp", "fsdp", None, None),
        P("tp", "fsdp", None, None),
        P("tp", None),
        P("tp", None),
        P("tp", None),
        P("tp", None),
    )
    out_specs = (
        P("fsdp", "tp"),
        P("fsdp", "tp"),
        P("tp", "fsdp", None, None),
        P("tp", "fsdp", None, None),
        P("tp", "fsdp", None, None),
    )
    return jax.shard_map(
        on_device, mesh=mesh, in_specs=in_specs, out_specs=out_specs, check_vma=False
    )
```

```python
import functools

import jax
import jax.numpy as jnp
from jax import lax
from jax.experimental import pallas as pl
from jax.experimental.pallas import tpu as pltpu
from jax.sharding import PartitionSpec as P

RING = 4
CHUNKS = 2
F32 = jnp.float32
BF16 = jnp.bfloat16
NT = (((1,), (1,)), ((), ()))
TN = (((0,), (0,)), ((), ()))


def up32(ref, *idx):
    return ref[idx].astype(F32)


def kernel(
    x_hbm, og_hbm, gt_hbm, ut_hbm, dt_hbm, rows_in_hbm, cols_in_hbm, rows_dn_hbm, cols_dn_hbm,
    out_ref, grad_ref,
    x, og, tg, tu, td, wgu, wd, hid, act, gb, pp, part, rc, r1r, r1f, q2, r2r, r2f, gr, rzr, rzf,
    lists, inv_in, inv_dn,
    lsem, ags, agr, cs, cr, s1s, s1r, s2s, s2r, zs, zr,
):
    z = lax.axis_index("fsdp")
    t = lax.axis_index("tp")
    core = lax.rem(t, 2)
    chip = t // 2
    px = lax.rem(chip, RING)
    py = chip // RING
    tok = x.shape[1]
    blk = tg.shape[1]
    n_tiles = tg.shape[0] - 1
    row_blocks = x.shape[0]
    col_blocks = wd.shape[0] // blk
    per = n_tiles // RING
    ct = tok // CHUNKS
    ht = ct // 4

    def wrap(v):
        return lax.rem(v + RING, RING)

    def dev(zz, yy, xx, cc):
        return (zz, (yy * RING + xx) * 2 + cc)

    def nbr(axis, step):
        if axis == "x":
            return dev(z, py, wrap(px + step), core)
        if axis == "y":
            return dev(z, wrap(py + step), px, core)
        return dev(wrap(z + step), py, px, core)

    partner = dev(z, py, px, 1 - core)
    pos = {"x": px, "y": py, "z": z}
    axes = (("x", "y"), ("y", "x"))

    def remote(src, dst, ss, rs, to):
        return pltpu.make_async_remote_copy(
            src_ref=src, dst_ref=dst, send_sem=ss, recv_sem=rs,
            device_id=to, device_id_type=pl.DeviceIdType.MESH,
        )

    sends = []

    def send(src, dst, ss, rs, to):
        c = remote(src, dst, ss, rs, to)
        c.start()
        sends.append(c)

    tiles_hbm = (gt_hbm, ut_hbm, dt_hbm)
    tiles = (tg, tu, td)
    own = pl.ds(z * per, per)
    loads = [
        pltpu.make_async_copy(tiles_hbm[m].at[0], tiles[m].at[own], lsem.at[m]) for m in range(3)
    ]
    for c in loads:
        c.start()

    lists_hbm = (rows_in_hbm, cols_in_hbm, rows_dn_hbm, cols_dn_hbm)
    list_loads = [
        pltpu.make_async_copy(lists_hbm[j].at[0], lists.at[j], lsem.at[5 + j]) for j in range(4)
    ]
    for c in list_loads:
        c.start()

    barrier = pltpu.get_barrier_semaphore()
    everyone = [partner] + [nbr(a, s) for a in "xyz" for s in (1, -1)]
    for to in everyone:
        pl.semaphore_signal(barrier, inc=1, device_id=to, device_id_type=pl.DeviceIdType.MESH)
    pl.semaphore_wait(barrier, len(everyone))

    def ag_own(m):
        for d, step in enumerate((1, -1)):
            send(tiles_hbm[m].at[0], tiles[m].at[own], ags.at[m, d], agr.at[m, d], nbr("z", step))

    def ag_wait(m, d):
        slot = tiles[m].at[pl.ds(wrap(z - 1 if d == 0 else z + 1) * per, per)]
        remote(slot, slot, ags.at[m, d], agr.at[m, d], partner).wait_recv()

    half = per // 2

    def ag_relay(m):
        for d, step in enumerate((1, -1)):
            ag_wait(m, d)
            piece = tiles[m].at[pl.ds(wrap(z - step) * per + d * half, half)]
            send(piece, piece, ags.at[m, 2 + d], agr.at[m, 2 + d], nbr("z", step))

    def ag_last(m):
        for d in range(2):
            piece = tiles[m].at[pl.ds(wrap(z + 2) * per + d * half, half)]
            remote(piece, piece, ags.at[m, 2 + d], agr.at[m, 2 + d], partner).wait_recv()

    for m in range(3):
        ag_own(m)

    def load_block(r, carry):
        cols = pl.ds(r * blk, blk)
        pltpu.make_async_copy(x_hbm.at[:, cols], x.at[r], lsem.at[3]).start()
        pltpu.make_async_copy(og_hbm.at[:, cols], og.at[r], lsem.at[4]).start()
        return carry

    lax.fori_loop(0, row_blocks, load_block, 0)

    for c in list_loads:
        c.wait()
    keys_in = [lists[0, k] * col_blocks + lists[1, k] for k in range(n_tiles)]
    keys_dn = [lists[2, k] * row_blocks + lists[3, k] for k in range(n_tiles)]

    def table(i, carry):
        v = jnp.int32(n_tiles)
        w = jnp.int32(n_tiles)
        for k in range(n_tiles):
            v = jnp.where(keys_in[k] == i, jnp.int32(k), v)
            w = jnp.where(keys_dn[k] == i, jnp.int32(k), w)
        inv_in[i] = v
        inv_dn[i] = w
        return carry

    lax.fori_loop(0, row_blocks * col_blocks, table, 0)
    for m in range(3):
        tiles[m][n_tiles] = jnp.zeros((blk, blk), BF16)

    for m in range(3):
        ag_relay(m)

    pairs = row_blocks // 2

    def place(j):
        return pl.ds((lax.rem(j, 2) * pairs + j // 2) * blk, blk)

    def build_in(m):
        def step(r, carry):
            rows = place(r)
            for c in range(col_blocks):
                c0 = (2 * c + m) * blk
                wgu[rows, c0:c0 + blk] = tiles[m][inv_in[r * col_blocks + c]]
            return carry

        loads[m].wait()
        ag_last(m)
        lax.fori_loop(0, row_blocks, step, 0)

    build_in(0)
    build_in(1)
    pltpu.make_async_copy(x, x, lsem.at[3]).wait()

    by_core = [2 * i + cc for cc in range(2) for i in range(pairs)]

    def wide(ref, rows, order):
        return jnp.concatenate([ref[r, rows] for r in order], axis=1)

    def forward(k):
        rows = pl.ds(k * ct, ct)

        def step(c, carry):
            cols = pl.ds(c * 2 * blk, 2 * blk)
            h = jnp.dot(wide(x, rows, by_core), wgu[:, cols], preferred_element_type=F32)
            hid[rows, cols] = h
            gate = h[:, :blk]
            act[c, rows] = (gate * jax.nn.sigmoid(gate) * h[:, blk:]).astype(BF16)
            return carry

        lax.fori_loop(0, col_blocks, step, 0)

    def build_dn(j, carry):
        cols = place(j)
        for c in range(col_blocks):
            wd[c * blk:(c + 1) * blk, cols] = td[inv_dn[c * row_blocks + j]]
        return carry

    def down_ready():
        loads[2].wait()
        pltpu.make_async_copy(og, og, lsem.at[4]).wait()
        ag_last(2)
        lax.fori_loop(0, row_blocks, build_dn, 0)

    def recv(ref, ss, rs):
        remote(ref, ref, ss, rs, partner).wait_recv()

    def half_part(i, mine, product):
        cc = core if mine else 1 - core

        def step(yh, carry):
            for ye in range(2):
                yy = yh * 2 + ye
                for xp in range(2):
                    val = product(pl.ds((cc * pairs + yy * RING + xp * 2) * blk, 2 * blk))
                    for xe in range(2):
                        xx = xp * 2 + xe
                        for a, (d1, d2) in enumerate(((xx, yy), (yy, xx))):
                            for h in range(2):
                                r0 = (a * 2 + h) * ht
                                v = val[r0:r0 + ht, xe * blk:(xe + 1) * blk]
                                if mine:
                                    v = v + rc[i, a, d1, h, d2].astype(F32)
                                    part[i, a, d1, h, d2] = v.astype(BF16)
                                else:
                                    pp[i, a, d1, h, d2] = v.astype(BF16)
            return carry

        if mine:
            for a in range(2):
                recv(rc.at[i, a], cs.at[i, a], cr.at[i, a])
        lax.fori_loop(0, RING // 2, step, 0)
        if not mine:
            for a in range(2):
                send(pp.at[i, a], rc.at[i, a], cs.at[i, a], cr.at[i, a], partner)

    def out_part(k, mine):
        lhs = wide(act, pl.ds(k * ct, ct), range(col_blocks))
        half_part(
            k, mine, lambda f: jnp.dot(lhs, wd[:, f], preferred_element_type=F32)
        )

    def in_part(k, mine):
        lhs = wide(gb, pl.ds(k * ct, ct), range(col_blocks))
        half_part(
            CHUNKS + k, mine,
            lambda f: lax.dot_general(lhs, wgu[f, :], NT, preferred_element_type=F32),
        )

    def ev_a(i):
        for d, s in enumerate((1, -1)):
            for a in range(2):
                ax = axes[a][0]
                e = i * 2 + a
                send(
                    part.at[i, a, wrap(pos[ax] + 2), d], r1r.at[e, d], s1s.at[e, d],
                    s1r.at[e, d], nbr(ax, s),
                )
        for d, s in enumerate((1, -1)):
            for a in range(2):
                ax = axes[a][0]
                e = i * 2 + a
                send(
                    part.at[i, a, wrap(pos[ax] + s), 1 - d], r1f.at[e, d, 1 - d],
                    s1s.at[e, 2 + d], s1r.at[e, 2 + d], nbr(ax, s),
                )

    def ev_b(i):
        for a in range(2):
            ax = axes[a][0]
            p = pos[ax]
            e = i * 2 + a
            for d, s in enumerate((1, -1)):
                q = wrap(p + s)
                recv(r1r.at[e, d], s1s.at[e, d], s1r.at[e, d])
                part[i, a, q, d] = (up32(part, i, a, q, d) + up32(r1r, e, d)).astype(BF16)
                send(
                    part.at[i, a, q, d], r1f.at[e, d, d], s1s.at[e, 4 + d],
                    s1r.at[e, 4 + d], nbr(ax, s),
                )

    def ev_c(i):
        for a in range(2):
            ax, ax2 = axes[a]
            p = pos[ax]
            q = pos[ax2]
            e = i * 2 + a
            for d in range(2):
                recv(r1f.at[e, d, 1 - d], s1s.at[e, 2 + d], s1r.at[e, 2 + d])
                recv(r1f.at[e, d, d], s1s.at[e, 4 + d], s1r.at[e, 4 + d])
            for h in range(2):
                val = (
                    up32(part, i, a, p, h) + up32(r1f, e, 0, h) + up32(r1f, e, 1, h)
                ).astype(BF16)
                for d2 in range(RING):
                    q2[e, d2, h] = val[d2]
            far = wrap(q + 2)
            for d, s in enumerate((1, -1)):
                send(q2.at[e, far, d], r2r.at[e, d], s2s.at[e, d], s2r.at[e, d], nbr(ax2, s))
            for d, s in enumerate((1, -1)):
                send(
                    q2.at[e, wrap(q + s), 1 - d], r2f.at[e, d, 1 - d], s2s.at[e, 2 + d],
                    s2r.at[e, 2 + d], nbr(ax2, s),
                )

    def ev_d(i):
        for a in range(2):
            ax2 = axes[a][1]
            q = pos[ax2]
            e = i * 2 + a
            for d, s in enumerate((1, -1)):
                w = wrap(q + s)
                recv(r2r.at[e, d], s2s.at[e, d], s2r.at[e, d])
                q2[e, w, d] = (up32(q2, e, w, d) + up32(r2r, e, d)).astype(BF16)
                send(
                    q2.at[e, w, d], r2f.at[e, d, d], s2s.at[e, 4 + d], s2r.at[e, 4 + d],
                    nbr(ax2, s),
                )

    def ev_e(i):
        for a in range(2):
            q = pos[axes[a][1]]
            e = i * 2 + a
            for d in range(2):
                recv(r2f.at[e, d, 1 - d], s2s.at[e, 2 + d], s2r.at[e, 2 + d])
                recv(r2f.at[e, d, d], s2s.at[e, 4 + d], s2r.at[e, 4 + d])
            for h in range(2):
                r0 = (i % CHUNKS) * ct + (a * 2 + h) * ht
                out_ref[i // CHUNKS, r0:r0 + ht, :] = (
                    up32(q2, e, q, h) + up32(r2f, e, 0, h) + up32(r2f, e, 1, h)
                ).astype(BF16)

    def ev_z0():
        far = wrap(z + 2)
        grads(far)
        for d, s in enumerate((1, -1)):
            send(gr.at[far, d], rzr.at[d], zs.at[d], zr.at[d], nbr("z", s))

    def ev_zp():
        for d, s in enumerate((1, -1)):
            grads(wrap(z + s))
            send(gr.at[wrap(z + s), 1 - d], rzf.at[d, 1 - d], zs.at[2 + d], zr.at[2 + d], nbr("z", s))

    def ev_z1():
        for d, s in enumerate((1, -1)):
            q = wrap(z + s)
            recv(rzr.at[d], zs.at[d], zr.at[d])
            gr[q, d] = (up32(gr, q, d) + up32(rzr, d)).astype(BF16)
            send(gr.at[q, d], rzf.at[d, d], zs.at[4 + d], zr.at[4 + d], nbr("z", s))

    def ev_z2():
        for d in range(2):
            recv(rzf.at[d, 1 - d], zs.at[2 + d], zr.at[2 + d])
            recv(rzf.at[d, d], zs.at[4 + d], zr.at[4 + d])
        for h in range(2):
            for m in range(3):
                for e in range(half):
                    grad_ref[m, h * half + e] = (
                        up32(gr, z, h, m, e) + up32(rzf, 0, h, m, e) + up32(rzf, 1, h, m, e)
                    )

    def back(k):
        rows = pl.ds(k * ct, ct)

        def step(n, carry):
            ag = lax.dot_general(
                wide(og, rows, by_core), wd[pl.ds(n * 2 * blk, 2 * blk), :], NT, preferred_element_type=F32
            )
            for e in range(2):
                c = n * 2 + e
                c0 = c * 2 * blk
                gate = hid[rows, pl.ds(c0, blk)]
                up = hid[rows, pl.ds(c0 + blk, blk)]
                a = ag[:, e * blk:(e + 1) * blk]
                s = jax.nn.sigmoid(gate)
                gb[c, rows, :blk] = (a * up * s * (1.0 + gate * (1.0 - s))).astype(BF16)
                gb[c, rows, blk:] = (a * (gate * s)).astype(BF16)
            return carry

        lax.fori_loop(0, col_blocks // 2, step, 0)

    def grads(d):
        for j in range(per):
            k = d * per + j
            h, e = j // half, j % half
            g = lax.dot_general(
                x[lists[0, k]], gb[lists[1, k]], TN, preferred_element_type=F32
            ).astype(BF16)
            gr[d, h, 0, e] = g[:, :blk]
            gr[d, h, 1, e] = g[:, blk:]
            gr[d, h, 2, e] = lax.dot_general(
                act[lists[2, k]], og[lists[3, k]], TN, preferred_element_type=F32
            ).astype(BF16)

    forward(0)
    down_ready()
    out_part(0, False)
    forward(1)
    out_part(1, False)
    out_part(0, True)
    ev_a(0)
    back(0)
    out_part(1, True)
    ev_a(1)
    in_part(0, False)
    ev_b(0)
    back(1)
    in_part(0, True)
    ev_a(2)
    in_part(1, False)
    ev_b(1)
    ev_z0()
    ev_c(0)
    in_part(1, True)
    ev_a(3)
    ev_zp()
    ev_b(2)
    ev_c(1)
    ev_d(0)
    grads(z)
    ev_b(3)
    ev_z1()
    ev_d(1)
    ev_c(2)
    ev_e(0)
    ev_c(3)
    ev_e(1)
    ev_d(2)
    ev_z2()
    ev_d(3)
    ev_e(2)
    ev_e(3)
    for c in sends:
        c.wait_send()


def finish(sums, tile_sums, ffn_ref, ing_ref, gg_ref, ug_ref, dg_ref):
    ffn_ref[...] = sums[0]
    ing_ref[...] = sums[1]
    for m, ref in enumerate((gg_ref, ug_ref, dg_ref)):
        ref[0] = tile_sums[m]


def on_device(
    inputs, out_grad, gate_tiles, up_tiles, down_tiles, in_rows, in_cols, down_rows, down_cols
):
    tok, width = inputs.shape
    blk = gate_tiles.shape[2]
    n_tiles = in_rows.shape[1]
    row_blocks = width // blk
    hidden = n_tiles * blk // 4
    steps = 2 * CHUNKS
    ht = tok // (CHUNKS * 4)
    half = n_tiles // RING // 2
    ev = steps * 2
    any_spec = pl.BlockSpec(memory_space=pl.ANY)
    vmem = pl.BlockSpec(memory_space=pltpu.VMEM)
    dma = pltpu.SemaphoreType.DMA
    entries = row_blocks * hidden // blk
    sums, tile_sums = pl.pallas_call(
        kernel,
        out_shape=(
            jax.ShapeDtypeStruct((2, tok, blk), BF16),
            jax.ShapeDtypeStruct((3,) + gate_tiles.shape[1:], F32),
        ),
        in_specs=[any_spec] * 9,
        out_specs=[vmem] * 2,
        scratch_shapes=[
            pltpu.VMEM((row_blocks, tok, blk), BF16),
            pltpu.VMEM((row_blocks, tok, blk), BF16),
            pltpu.VMEM((n_tiles + 1, blk, blk), BF16),
            pltpu.VMEM((n_tiles + 1, blk, blk), BF16),
            pltpu.VMEM((n_tiles + 1, blk, blk), BF16),
            pltpu.VMEM((width, 2 * hidden), BF16),
            pltpu.VMEM((hidden, width), BF16),
            pltpu.VMEM((tok, 2 * hidden), F32),
            pltpu.VMEM((hidden // blk, tok, blk), BF16),
            pltpu.VMEM((hidden // blk, tok, 2 * blk), BF16),
            pltpu.VMEM((steps, 2, RING, 2, RING, ht, blk), BF16),
            pltpu.VMEM((steps, 2, RING, 2, RING, ht, blk), BF16),
            pltpu.VMEM((steps, 2, RING, 2, RING, ht, blk), BF16),
            pltpu.VMEM((ev, 2, RING, ht, blk), BF16),
            pltpu.VMEM((ev, 2, 2, RING, ht, blk), BF16),
            pltpu.VMEM((ev, RING, 2, ht, blk), BF16),
            pltpu.VMEM((ev, 2, ht, blk), BF16),
            pltpu.VMEM((ev, 2, 2, ht, blk), BF16),
            pltpu.VMEM((RING, 2, 3, half, blk, blk), BF16),
            pltpu.VMEM((2, 3, half, blk, blk), BF16),
            pltpu.VMEM((2, 2, 3, half, blk, blk), BF16),
            pltpu.SMEM((4, n_tiles), jnp.int32),
            pltpu.SMEM((entries,), jnp.int32),
            pltpu.SMEM((entries,), jnp.int32),
            dma((9,)),
            dma((3, 4)),
            dma((3, 4)),
            dma((steps, 2)),
            dma((steps, 2)),
            dma((ev, 6)),
            dma((ev, 6)),
            dma((ev, 6)),
            dma((ev, 6)),
            dma((6,)),
            dma((6,)),
        ],
        compiler_params=pltpu.CompilerParams(
            collective_id=0, has_side_effects=True, vmem_limit_bytes=60 * 1024 * 1024
        ),
    )(inputs, out_grad, gate_tiles, up_tiles, down_tiles, in_rows, in_cols, down_rows, down_cols)
    return pl.pallas_call(
        finish,
        out_shape=(jax.ShapeDtypeStruct((tok, blk), BF16),) * 2
        + (jax.ShapeDtypeStruct(gate_tiles.shape, F32),) * 3,
        in_specs=[vmem] * 2,
        out_specs=[vmem] * 5,
    )(sums, tile_sums)


def solution(mesh):
    in_specs = (
        P("fsdp", None),
        P("fsdp", None),
        P("tp", "fsdp", None, None),
        P("tp", "fsdp", None, None),
        P("tp", "fsdp", None, None),
        P("tp", None),
        P("tp", None),
        P("tp", None),
        P("tp", None),
    )
    out_specs = (
        P("fsdp", "tp"),
        P("fsdp", "tp"),
        P("tp", "fsdp", None, None),
        P("tp", "fsdp", None, None),
        P("tp", "fsdp", None, None),
    )
    return jax.shard_map(
        on_device, mesh=mesh, in_specs=in_specs, out_specs=out_specs, check_vma=False
    )
```
